32 devices in a mesh: dp: 16 (over z, x, core), tensor: 2 (over y).
Axes of the slice: x: 2, y: 2, z: 4, core: 2. Of those that a mesh axis runs over, the one named last changes fastest.
Arguments:
- tokens: bfloat16 [2048, 768], P('dp'), may hold values from -6 to 6
- seg_ids: int32 [2048], P('dp'), may hold values from -1 to 6, as said below
- query_weight: bfloat16 [768, 768], P(None, 'tensor'), may hold values from -0.21875 to 0.21875
- key_weight: bfloat16 [768, 768], P(None, 'tensor'), may hold values from -0.21875 to 0.21875
- value_weight: bfloat16 [768, 768], P(None, 'tensor'), may hold values from -0.21875 to 0.21875
- query_bias: float32 [768], P('tensor'), may hold values from -3 to 3
- value_bias: float32 [768], P('tensor'), may hold values from -3 to 3
- out_weight: bfloat16 [768, 768], P(None, 'tensor'), may hold values from -1.75 to 1.75
- out_bias: float32 [768], replicated, may hold values from -3 to 3
- attention_norm_gain: float32 [768], replicated, may hold values from 0.25 to 1.75
- attention_norm_shift: float32 [768], replicated, may hold values from -3 to 3
- up_weight: bfloat16 [768, 3072], P(None, 'tensor'), may hold values from -0.21875 to 0.21875
- up_bias: float32 [3072], P('tensor'), may hold values from -3 to 3
- down_weight: bfloat16 [768, 3072], P(None, 'tensor'), may hold values from -0.109375 to 0.109375
- down_bias: float32 [768], replicated, may hold values from -3 to 3
- feedforward_norm_gain: float32 [768], replicated, may hold values from 0.25 to 1.75
- feedforward_norm_shift: float32 [768], replicated, may hold values from -3 to 3
- cotangent: bfloat16 [2048, 768], P('dp'), may hold values from -6 to 6
Outputs:
- mixed: bfloat16 [2048, 768], P('dp')
- grad_tokens: float32 [2048, 768], P('dp')
- grad_query_weight: float32 [768, 768], P('dp', 'tensor')
- grad_key_weight: float32 [768, 768], P('dp', 'tensor')
- grad_value_weight: float32 [768, 768], P('dp', 'tensor')
- grad_query_bias: float32 [768], P('tensor')
- grad_value_bias: float32 [768], P('tensor')
- grad_out_weight: float32 [768, 768], P('dp', 'tensor')
- grad_out_bias: float32 [768], replicated
- grad_gain_first: float32 [768], replicated
- grad_shift_first: float32 [768], replicated
- grad_up_weight: float32 [768, 3072], P('dp', 'tensor')
- grad_up_bias: float32 [3072], P('tensor')
- grad_down_weight: float32 [768, 3072], P('dp', 'tensor')
- grad_down_bias: float32 [768], replicated
- grad_gain_second: float32 [768], replicated
- grad_shift_second: float32 [768], replicated
The draws below stay inside these ranges and needn't reach their ends.
Inputs may be any that keep to these rules, and one draw needn't show every extreme that they name: `seg_ids`: within each device's block of 128 tokens the ids are 0, 1, 2, ... in order, one for each packed sequence of 16 to 127 tokens, and -1 marks the padding from the last sequence's end to the block's end; the block's last token is always padding. Some block holds the most sequences that fit, and some block one sequence of 127 tokens.
All inputs are finite; a program needn't handle non-finite values.
Results may differ from the reference program's by a relative error of at most 0.013.
Values sent between devices are 32-bit elements; how exact they have to be, the bound alone decides.
A program may use at most 128 MiB of HBM per device.

```python
import math
import jax
import jax.numpy as jnp
from jax import lax

D = 768
HEADS = 12
HEAD_DIM = 64
FF = 3072
TOK_DEV = 128
MINSEQ = 16
TOKENS = 2048


def draw_seg_ids(key, part):
    device_count = TOKENS // TOK_DEV
    slots = TOK_DEV // MINSEQ + 1
    lengths = jax.random.randint(key, (device_count, slots), MINSEQ, TOK_DEV)
    ends = jnp.cumsum(lengths, axis=1)
    kept = ends < TOK_DEV
    positions = jnp.arange(TOK_DEV)
    finished = jnp.sum((kept[:, None, :] & (ends[:, None, :] <= positions[None, :, None])).astype(jnp.int32), axis=2)
    last_end = jnp.max(jnp.where(kept, ends, 0), axis=1)
    ids = jnp.where(positions[None, :] < last_end[:, None], finished, -1)
    most_count = (TOK_DEV - 1) // MINSEQ
    packed_row = jnp.where(positions < most_count * MINSEQ, positions // MINSEQ, -1)
    long_row = jnp.where(positions < TOK_DEV - 1, 0, -1)
    rows = jnp.arange(device_count)[:, None]
    ids = jnp.where(rows == 0, packed_row[None, :], ids)
    ids = jnp.where(rows == 1, long_row[None, :], ids)
    return ids.reshape(TOKENS).astype(jnp.int32)


def strengthened(values, key, source, target, shards_of, factor):
    def block_of(dim):
        return (jnp.arange(values.shape[dim]) // (values.shape[dim] // shards_of)).reshape((-1,) + (1,) * (values.ndim - 1 - dim))

    near = jax.random.permutation(key, shards_of)[block_of(target)]
    other_side = (block_of(target) + shards_of // 2) % shards_of
    return jnp.where((block_of(source) == near) | (block_of(source) == other_side), factor * values, values)


def block_scale(stream_key, shape, split, smallest, largest):
    def one(position, parts):
        steps = jax.random.uniform(jax.random.fold_in(jax.random.fold_in(stream_key, 6), position), (parts,), jnp.float32, smallest / len(split), largest / len(split))
        return jnp.repeat(jnp.exp(steps), shape[position] // parts).reshape((-1,) + (1,) * (len(shape) - position - 1))

    level = one(*split[0])
    for cut in split[1:]:
        level = level * one(*cut)
    return level


def scatter_about(own_key, dims, scale, bound, split=(), kind=jnp.bfloat16):
    entries = jax.random.normal(own_key, dims, jnp.float32) * scale
    if len(split) > 0:
        entries = block_scale(own_key, dims, split, -0.22, 0.18) * entries
    return jnp.clip(entries, min=-bound, max=bound).astype(kind)


def noise_with(key, dims, spread, limit, split, heavy, dtype=jnp.bfloat16):
    values = spread * jax.random.normal(key, dims, jnp.float32)
    if split:
        values = values * block_scale(key, dims, split, -0.22, 0.18)
    return jnp.clip(strengthened(values, jax.random.fold_in(key, 3), *heavy), -limit, limit).astype(dtype)


def setup_inputs(seed: int = 0) -> dict:
    arg_keys = jax.random.split(jax.random.key(seed), 19)
    return {
        "tokens": noise_with(arg_keys[0], (TOKENS, D), 1.0, 6.0, ((0, 16),), (0, 1, 16, 2.0)),
        "seg_ids": draw_seg_ids(jax.random.fold_in(arg_keys[18], 71), 0),
        "query_weight": scatter_about(arg_keys[2], (D, D), D ** -0.5, 0.21875, ((1, 2),)),
        "key_weight": scatter_about(arg_keys[3], (D, D), D ** -0.5, 0.21875, ((1, 2),)),
        "value_weight": scatter_about(arg_keys[4], (D, D), D ** -0.5, 0.21875, ((1, 2),)),
        "query_bias": scatter_about(arg_keys[5], (D,), 0.5, 3.0, ((0, 2),), jnp.float32),
        "value_bias": scatter_about(arg_keys[6], (D,), 0.5, 3.0, ((0, 2),), jnp.float32),
        "out_weight": scatter_about(arg_keys[7], (D, D), (max(2 * D // TOK_DEV, 1)) ** -0.5, 1.75, ((1, 2),)),
        "out_bias": scatter_about(arg_keys[8], (D,), 0.5, 3.0, (), jnp.float32),
        "attention_norm_gain": jnp.clip(1.0 + 0.15 * jax.random.normal(arg_keys[9], (D,), jnp.float32), 0.25, 1.75),
        "attention_norm_shift": scatter_about(arg_keys[10], (D,), 0.5, 3.0, (), jnp.float32),
        "up_weight": scatter_about(arg_keys[11], (D, FF), D ** -0.5, 0.21875, ((1, 2),)),
        "up_bias": scatter_about(arg_keys[12], (FF,), 0.5, 3.0, ((0, 2),), jnp.float32),
        "down_weight": scatter_about(arg_keys[13], (D, FF), FF ** -0.5, 0.109375, ((1, 2),)),
        "down_bias": scatter_about(arg_keys[14], (D,), 0.5, 3.0, (), jnp.float32),
        "feedforward_norm_gain": jnp.clip(1.0 + 0.15 * jax.random.normal(arg_keys[15], (D,), jnp.float32), 0.25, 1.75),
        "feedforward_norm_shift": scatter_about(arg_keys[16], (D,), 0.5, 3.0, (), jnp.float32),
        "cotangent": noise_with(arg_keys[17], (TOKENS, D), 1.0, 6.0, ((0, 16),), (0, 1, 16, 2.0)),
    }


@jax.custom_vjp
def low(v):
    return lax.optimization_barrier(v.astype(jnp.bfloat16)).astype(jnp.float32)

@jax.custom_vjp
def low_back(v):
    return v

def low_keep(v):
    return (low(v), None)

def low_pass(kept, grad):
    return (grad,)

def back_keep(v):
    return (v, None)

def back_low(kept, grad):
    return (low(grad),)
low.defvjp(low_keep, low_pass)
low_back.defvjp(back_keep, back_low)
epsilon = 1e-12
masked_value = -1e+30
highest = lax.Precision.HIGHEST

def matmul(left, right):
    return jnp.dot(left, right, precision=highest, preferred_element_type=jnp.float32)

def layer_norm(rows, norm_gain, shift):
    row_mean = lax.optimization_barrier(jnp.mean(rows, axis=-1, keepdims=True))
    centred = rows - row_mean
    variance = lax.optimization_barrier(jnp.mean(centred * centred, axis=-1, keepdims=True))
    return centred * lax.rsqrt(variance + epsilon) * norm_gain + shift

def attend(queries, key_rows, value_rows, seg_ids):
    key_count = key_rows.shape[0]
    block_rows = min(512, key_count)
    block_count = key_count // block_rows
    key_heads = key_rows.reshape(key_count, HEADS, HEAD_DIM)
    value_heads = value_rows.reshape(key_count, HEADS, HEAD_DIM)
    score_scale = 1.0 / math.sqrt(HEAD_DIM)

    def one_block(block_item):
        query_block, block_ids = block_item
        query_heads = query_block.reshape(block_rows, HEADS, HEAD_DIM)
        scores = jnp.einsum('qhe,khe->hqk', query_heads, key_heads, precision=highest) * score_scale
        scores = low_back(scores)
        allowed = (block_ids[:, None] == seg_ids[None, :])[None]
        scores = jnp.where(allowed, scores, masked_value)
        row_max = lax.optimization_barrier(jnp.max(scores, axis=2, keepdims=True))
        weights_exp = jnp.exp(scores - row_max)
        probabilities = low(weights_exp / lax.optimization_barrier(jnp.sum(weights_exp, axis=2, keepdims=True)))
        context = jnp.einsum('hqk,khe->qhe', probabilities, value_heads, precision=highest)
        return context.reshape(block_rows, HEADS * HEAD_DIM)
    contexts = lax.map(jax.checkpoint(one_block), (queries.reshape(block_count, block_rows, HEADS * HEAD_DIM), seg_ids.reshape(block_count, block_rows)))
    return contexts.reshape(key_count, HEADS * HEAD_DIM)

def forward(tokens, seg_ids, query_weight, key_weight, value_weight, query_bias, value_bias, out_weight, out_bias, attention_norm_gain, attention_norm_shift, up_weight, up_bias, down_weight, down_bias, feedforward_norm_gain, feedforward_norm_shift):
    queries = low(low_back(matmul(tokens, query_weight) + query_bias))
    key_rows = low(low_back(matmul(tokens, key_weight)))
    value_rows = low(low_back(matmul(tokens, value_weight) + value_bias))
    context = low(low_back(attend(queries, key_rows, value_rows, seg_ids)))
    attn = low_back(matmul(context, out_weight.T) + out_bias)
    hidden_state = layer_norm(tokens + attn, attention_norm_gain, attention_norm_shift)
    up_rows = low_back(matmul(low(hidden_state), up_weight) + up_bias)
    act = low(jax.nn.gelu(up_rows, approximate=False))
    down = low_back(matmul(act, down_weight.T) + down_bias)
    normed = layer_norm(hidden_state + down, feedforward_norm_gain, feedforward_norm_shift)
    return jnp.where((seg_ids >= 0)[:, None], normed, 0.0)

def reference(tokens, seg_ids, query_weight, key_weight, value_weight, query_bias, value_bias, out_weight, out_bias, attention_norm_gain, attention_norm_shift, up_weight, up_bias, down_weight, down_bias, feedforward_norm_gain, feedforward_norm_shift, cotangent):
    params = tuple((item.astype(jnp.float32) for item in (query_weight, key_weight, value_weight, query_bias, value_bias, out_weight, out_bias, attention_norm_gain, attention_norm_shift, up_weight, up_bias, down_weight, down_bias, feedforward_norm_gain, feedforward_norm_shift)))
    block_count = TOKENS // TOK_DEV
    inputs = tokens.astype(jnp.float32).reshape(block_count, TOK_DEV, D)
    id_blocks = seg_ids.reshape(block_count, TOK_DEV)
    cot_blocks = cotangent.astype(jnp.float32).reshape(block_count, TOK_DEV, D)

    def step(sums, block_item):
        block_tokens, block_ids, block_cot = block_item

        def local(inputs_block, *weights):
            return forward(inputs_block, block_ids, *weights)
        outputs, pull = jax.vjp(local, block_tokens, *params)
        grads = pull(block_cot)
        sums = tuple((left + right for left, right in zip(sums, grads[1:])))
        return (sums, (outputs.astype(jnp.bfloat16), grads[0]))
    start = tuple((jnp.zeros_like(item) for item in params))
    sums, (mixed, grad_tokens) = lax.scan(step, start, (inputs, id_blocks, cot_blocks))
    return (mixed.reshape(TOKENS, D), grad_tokens.reshape(TOKENS, D), sums[0], sums[1], sums[2], sums[3], sums[4], sums[5], sums[6], sums[7], sums[8], sums[9], sums[10], sums[11], sums[12], sums[13], sums[14])
```

```python
import math

import jax
import jax.numpy as jnp
from jax import lax
from jax.sharding import PartitionSpec as P

HEAD_DIM = 64


epsilon = 1e-12
masked_value = -1e30


def dot_rows(left, right):
    return lax.dot_general(
        left, right, (((1,), (1,)), ((), ())), preferred_element_type=jnp.float32
    )


def dot_cols(left, right):
    return lax.dot_general(
        left, right, (((0,), (0,)), ((), ())), preferred_element_type=jnp.float32
    )


def tensor_sum(part):
    size = lax.axis_size("tensor")
    if size != 2:
        return lax.psum(part, "tensor")
    return part + lax.ppermute(part, "tensor", [(0, 1), (1, 0)])


def dp_sum(part):
    size = lax.axis_size("dp")
    if size & (size - 1):
        return lax.psum(part, "dp")
    step = 1
    while step < size:
        part = part + lax.ppermute(part, "dp", [(i, i ^ step) for i in range(size)])
        step *= 2
    return part


def dp_share(parts):
    widths = [part.shape[1] for part in parts]
    share = lax.psum_scatter(
        jnp.concatenate(parts, axis=1), "dp", scatter_dimension=0, tiled=True
    )
    shares, start = [], 0
    for width in widths:
        shares.append(share[:, start : start + width])
        start += width
    return shares


def apply_layer_norm(rows):
    row_mean = jnp.mean(rows, axis=1, keepdims=True)
    centred = rows - row_mean
    inverse_deviation = lax.rsqrt(jnp.mean(centred * centred, axis=1, keepdims=True) + epsilon)
    return (centred * inverse_deviation, inverse_deviation)


def norm_backward_pass(incoming_gradient, centered_rows, inverse_deviation, norm_gain):
    scaled_rows = incoming_gradient * norm_gain
    row_gradient = inverse_deviation * (
        scaled_rows
        - jnp.mean(scaled_rows, axis=1, keepdims=True)
        - centered_rows * jnp.mean(scaled_rows * centered_rows, axis=1, keepdims=True)
    )
    return (
        row_gradient,
        jnp.sum(incoming_gradient * centered_rows, axis=0),
        jnp.sum(incoming_gradient, axis=0),
    )


def attend_forward(queries, key_rows, value_rows, seg_ids, head_count, head_width):
    key_count = key_rows.shape[0]
    block_rows = min(512, key_count)
    block_count = key_count // block_rows
    key_heads = key_rows.reshape(key_count, head_count, head_width)
    value_heads = value_rows.reshape(key_count, head_count, head_width)
    score_scale = 1.0 / math.sqrt(head_width)

    def one_block(block_item):
        query_block, block_ids = block_item
        query_heads = query_block.reshape(block_rows, head_count, head_width)
        scores = (
            jnp.einsum("qhe,khe->hqk", query_heads, key_heads, preferred_element_type=jnp.float32)
            * score_scale
        )
        allowed = (block_ids[:, None] == seg_ids[None, :])[None]
        scores = jnp.where(allowed, scores, masked_value)
        row_max = jnp.max(scores, axis=2, keepdims=True)
        weights_exp = jnp.exp(scores - row_max)
        mass = jnp.sum(weights_exp, axis=2, keepdims=True)
        probabilities = (weights_exp / mass).astype(jnp.bfloat16)
        context = jnp.einsum(
            "hqk,khe->qhe", probabilities, value_heads, preferred_element_type=jnp.float32
        )
        return (
            context.reshape(block_rows, head_count * head_width).astype(jnp.bfloat16),
            (row_max + jnp.log(mass))[:, :, 0],
        )

    contexts, log_mass = lax.map(
        one_block,
        (
            queries.reshape(block_count, block_rows, head_count * head_width),
            seg_ids.reshape(block_count, block_rows),
        ),
    )
    return (contexts.reshape(key_count, head_count * head_width), log_mass)


def attend_backward(
    queries, key_rows, value_rows, seg_ids, log_mass, grad_context, head_count, head_width
):
    key_count = key_rows.shape[0]
    block_rows = min(512, key_count)
    block_count = key_count // block_rows
    key_heads = key_rows.reshape(key_count, head_count, head_width)
    value_heads = value_rows.reshape(key_count, head_count, head_width)
    score_scale = 1.0 / math.sqrt(head_width)

    def one_block(carry, block_item):
        grad_keys, grad_values = carry
        query_block, block_ids, block_mass, grad_block = block_item
        query_heads = query_block.reshape(block_rows, head_count, head_width)
        grad_heads = grad_block.reshape(block_rows, head_count, head_width)
        scores = (
            jnp.einsum("qhe,khe->hqk", query_heads, key_heads, preferred_element_type=jnp.float32)
            * score_scale
        )
        allowed = (block_ids[:, None] == seg_ids[None, :])[None]
        probabilities = jnp.where(allowed, jnp.exp(scores - block_mass[:, :, None]), 0.0)
        rounded = probabilities.astype(jnp.bfloat16)
        grad_values = grad_values + jnp.einsum(
            "hqk,qhe->khe", rounded, grad_heads, preferred_element_type=jnp.float32
        )
        grad_probs = jnp.einsum(
            "qhe,khe->hqk", grad_heads, value_heads, preferred_element_type=jnp.float32
        )
        grad_scores = probabilities * (
            grad_probs - jnp.sum(probabilities * grad_probs, axis=2, keepdims=True)
        )
        grad_scores = grad_scores.astype(jnp.bfloat16)
        grad_query = (
            jnp.einsum("hqk,khe->qhe", grad_scores, key_heads, preferred_element_type=jnp.float32)
            * score_scale
        )
        grad_keys = (
            grad_keys
            + jnp.einsum(
                "hqk,qhe->khe", grad_scores, query_heads, preferred_element_type=jnp.float32
            )
            * score_scale
        )
        return ((grad_keys, grad_values), grad_query.reshape(block_rows, head_count * head_width))

    empty = jnp.zeros((key_count, head_count, head_width), jnp.float32)
    (grad_keys, grad_values), grad_queries = lax.scan(
        one_block,
        (empty, empty),
        (
            queries.reshape(block_count, block_rows, head_count * head_width),
            seg_ids.reshape(block_count, block_rows),
            log_mass,
            grad_context.reshape(block_count, block_rows, head_count * head_width),
        ),
    )
    width = head_count * head_width
    return (
        grad_queries.reshape(key_count, width).astype(jnp.bfloat16),
        grad_keys.reshape(key_count, width).astype(jnp.bfloat16),
        grad_values.reshape(key_count, width).astype(jnp.bfloat16),
    )


def local(
    tokens,
    seg_ids,
    query_weight,
    key_weight,
    value_weight,
    query_bias,
    value_bias,
    out_weight,
    out_bias,
    attention_norm_gain,
    attention_norm_shift,
    up_weight,
    up_bias,
    down_weight,
    down_bias,
    feedforward_norm_gain,
    feedforward_norm_shift,
    cotangent,
):
    head_width = HEAD_DIM
    head_count = query_weight.shape[1] // head_width
    valid_token_mask = (seg_ids >= 0)[:, None]
    queries = (
        jnp.dot(tokens, query_weight, preferred_element_type=jnp.float32) + query_bias
    ).astype(jnp.bfloat16)
    key_rows = jnp.dot(tokens, key_weight, preferred_element_type=jnp.float32).astype(jnp.bfloat16)
    value_rows = (
        jnp.dot(tokens, value_weight, preferred_element_type=jnp.float32) + value_bias
    ).astype(jnp.bfloat16)
    context, log_mass = attend_forward(
        queries, key_rows, value_rows, seg_ids, head_count, head_width
    )
    attn_sum = tensor_sum(dot_rows(context, out_weight))
    attention_residual = tokens.astype(jnp.float32) + attn_sum + out_bias
    centered_rows_first, inverse_deviation_first = apply_layer_norm(attention_residual)
    hidden_state = centered_rows_first * attention_norm_gain + attention_norm_shift
    hidden_low = hidden_state.astype(jnp.bfloat16)
    up_rows = jnp.dot(hidden_low, up_weight, preferred_element_type=jnp.float32) + up_bias
    act_low = jax.nn.gelu(up_rows, approximate=False).astype(jnp.bfloat16)
    down_sum = tensor_sum(dot_rows(act_low, down_weight))
    feedforward_residual = hidden_state + down_sum + down_bias
    centered_rows_second, inverse_deviation_second = apply_layer_norm(feedforward_residual)
    mixed = jnp.where(
        valid_token_mask, centered_rows_second * feedforward_norm_gain + feedforward_norm_shift, 0.0
    ).astype(jnp.bfloat16)
    incoming_gradient = jnp.where(valid_token_mask, cotangent.astype(jnp.float32), 0.0)
    grad_res_two, grad_gain_second, grad_shift_second = norm_backward_pass(
        incoming_gradient, centered_rows_second, inverse_deviation_second, feedforward_norm_gain
    )
    grad_down_low = grad_res_two.astype(jnp.bfloat16)
    grad_down_bias = jnp.sum(grad_down_low, axis=0, dtype=jnp.float32)
    grad_down_weight = dot_cols(grad_down_low, act_low)
    grad_act = jnp.dot(grad_down_low, down_weight, preferred_element_type=jnp.float32)
    normal_cdf = 0.5 * (1.0 + lax.erf(up_rows * (1.0 / math.sqrt(2.0))))
    normal_density = jnp.exp(-0.5 * up_rows * up_rows) * (1.0 / math.sqrt(2.0 * math.pi))
    grad_up_low = (grad_act * (normal_cdf + up_rows * normal_density)).astype(jnp.bfloat16)
    grad_up_bias = jnp.sum(grad_up_low, axis=0, dtype=jnp.float32)
    grad_up_weight = dot_cols(hidden_low, grad_up_low)
    back_sum = tensor_sum(dot_rows(grad_up_low, up_weight))
    hidden_gradient = grad_res_two + back_sum
    grad_res_one, grad_gain_first, grad_shift_first = norm_backward_pass(
        hidden_gradient, centered_rows_first, inverse_deviation_first, attention_norm_gain
    )
    grad_attn_low = grad_res_one.astype(jnp.bfloat16)
    grad_out_bias = jnp.sum(grad_attn_low, axis=0, dtype=jnp.float32)
    grad_out_weight = dot_cols(grad_attn_low, context)
    grad_context = jnp.dot(grad_attn_low, out_weight, preferred_element_type=jnp.float32).astype(
        jnp.bfloat16
    )
    grad_queries, grad_keys, grad_values = attend_backward(
        queries, key_rows, value_rows, seg_ids, log_mass, grad_context, head_count, head_width
    )
    grad_query_bias = jnp.sum(grad_queries, axis=0, dtype=jnp.float32)
    grad_value_bias = jnp.sum(grad_values, axis=0, dtype=jnp.float32)
    grad_query_weight = dot_cols(tokens, grad_queries)
    grad_key_weight = dot_cols(tokens, grad_keys)
    grad_value_weight = dot_cols(tokens, grad_values)
    input_part = (
        dot_rows(grad_queries, query_weight)
        + dot_rows(grad_keys, key_weight)
        + dot_rows(grad_values, value_weight)
    )
    grad_tokens = grad_res_one + tensor_sum(input_part)
    down_share, up_share = dp_share([grad_down_weight, grad_up_weight])
    query_share, key_share, value_share, out_share = dp_share(
        [grad_query_weight, grad_key_weight, grad_value_weight, grad_out_weight]
    )
    rows = [
        grad_query_bias,
        grad_value_bias,
        grad_up_bias,
        grad_out_bias,
        grad_gain_first,
        grad_shift_first,
        grad_down_bias,
        grad_gain_second,
        grad_shift_second,
    ]
    sums, start = [], 0
    total = dp_sum(jnp.concatenate(rows))
    for row in rows:
        sums.append(total[start : start + row.shape[0]])
        start += row.shape[0]
    (
        query_bias_sum,
        value_bias_sum,
        up_bias_sum,
        out_bias_sum,
        gain_first_sum,
        shift_first_sum,
        down_bias_sum,
        gain_second_sum,
        shift_second_sum,
    ) = sums
    return (
        mixed,
        grad_tokens,
        query_share,
        key_share,
        value_share,
        query_bias_sum,
        value_bias_sum,
        out_share,
        out_bias_sum,
        gain_first_sum,
        shift_first_sum,
        up_share,
        up_bias_sum,
        down_share,
        down_bias_sum,
        gain_second_sum,
        shift_second_sum,
    )


def solution(mesh):
    return jax.shard_map(
        local,
        mesh=mesh,
        in_specs=(
            P("dp", None),
            P("dp"),
            P(None, "tensor"),
            P(None, "tensor"),
            P(None, "tensor"),
            P("tensor"),
            P("tensor"),
            P(None, "tensor"),
            P(),
            P(),
            P(),
            P(None, "tensor"),
            P("tensor"),
            P(None, "tensor"),
            P(),
            P(),
            P(),
            P("dp", None),
        ),
        out_specs=(
            P("dp", None),
            P("dp", None),
            P("dp", "tensor"),
            P("dp", "tensor"),
            P("dp", "tensor"),
            P("tensor"),
            P("tensor"),
            P("dp", "tensor"),
            P(),
            P(),
            P(),
            P("dp", "tensor"),
            P("tensor"),
            P("dp", "tensor"),
            P(),
            P(),
            P(),
        ),
        check_vma=False,
    )
```

```python
import math

import jax
import jax.numpy as jnp
from jax import lax
from jax.sharding import PartitionSpec as P

HEAD_DIM = 64


epsilon = 1e-12
masked_value = -1e30


def dot_rows(left, right):
    return lax.dot_general(
        left, right, (((1,), (1,)), ((), ())), preferred_element_type=jnp.float32
    )


def dot_cols(left, right):
    return lax.dot_general(
        left, right, (((0,), (0,)), ((), ())), preferred_element_type=jnp.float32
    )


def tensor_sum(part):
    size = lax.axis_size("tensor")
    if size != 2:
        return lax.psum(part, "tensor")
    return part + lax.ppermute(part, "tensor", [(0, 1), (1, 0)])


def dp_sum(part):
    size = lax.axis_size("dp")
    if size & (size - 1):
        return lax.psum(part, "dp")
    step = 1
    while step < size:
        part = part + lax.ppermute(part, "dp", [(i, i ^ step) for i in range(size)])
        step *= 2
    return part


def dp_share(left, right, order):
    size = lax.axis_size("dp")
    count = size.bit_length() - 1
    if size != 1 << count:
        return lax.psum_scatter(dot_cols(left, right), "dp", scatter_dimension=0, tiled=True)
    place = lax.axis_index("dp")
    tokens, width = right.shape
    rows = left.shape[1] // size
    axes = list(range(count - 1, -1, -1))
    part = left.T.reshape((2,) * count + (rows, tokens))
    for step, bit in enumerate(order(count)):
        axis = axes.index(bit)
        mine = (place >> bit) & 1
        send = lax.dynamic_index_in_dim(part, 1 - mine, axis, keepdims=False)
        keep = lax.dynamic_index_in_dim(part, mine, axis, keepdims=False)
        axes.remove(bit)
        if step == 0:
            shape = (2,) * len(axes) + (rows, width)
            send, keep = (
                jnp.dot(
                    half.reshape(-1, tokens), right, preferred_element_type=jnp.float32
                ).reshape(shape)
                for half in (send, keep)
            )
        got = lax.ppermute(send, "dp", [(i, i ^ (1 << bit)) for i in range(size)])
        part = keep + got
    return part


def upward(count):
    return list(range(count))


def rotated(count):
    return [0] + list(range(2, count)) + list(range(1, min(2, count)))


def dp_share_halves(left, right):
    middle = right.shape[1] // 2
    return jnp.concatenate(
        [
            dp_share(left, right[:, :middle], upward),
            dp_share(left, right[:, middle:], rotated),
        ],
        axis=1,
    )


def apply_layer_norm(rows):
    row_mean = jnp.mean(rows, axis=1, keepdims=True)
    centred = rows - row_mean
    inverse_deviation = lax.rsqrt(jnp.mean(centred * centred, axis=1, keepdims=True) + epsilon)
    return (centred * inverse_deviation, inverse_deviation)


def norm_backward_pass(incoming_gradient, centered_rows, inverse_deviation, norm_gain):
    scaled_rows = incoming_gradient * norm_gain
    row_gradient = inverse_deviation * (
        scaled_rows
        - jnp.mean(scaled_rows, axis=1, keepdims=True)
        - centered_rows * jnp.mean(scaled_rows * centered_rows, axis=1, keepdims=True)
    )
    return (
        row_gradient,
        jnp.sum(incoming_gradient * centered_rows, axis=0),
        jnp.sum(incoming_gradient, axis=0),
    )


def attend_forward(queries, key_rows, value_rows, seg_ids, head_count, head_width):
    key_count = key_rows.shape[0]
    block_rows = min(512, key_count)
    block_count = key_count // block_rows
    key_heads = key_rows.reshape(key_count, head_count, head_width)
    value_heads = value_rows.reshape(key_count, head_count, head_width)
    score_scale = 1.0 / math.sqrt(head_width)

    def one_block(block_item):
        query_block, block_ids = block_item
        query_heads = query_block.reshape(block_rows, head_count, head_width)
        scores = (
            jnp.einsum("qhe,khe->hqk", query_heads, key_heads, preferred_element_type=jnp.float32)
            * score_scale
        )
        allowed = (block_ids[:, None] == seg_ids[None, :])[None]
        scores = jnp.where(allowed, scores, masked_value)
        row_max = jnp.max(scores, axis=2, keepdims=True)
        weights_exp = jnp.exp(scores - row_max)
        mass = jnp.sum(weights_exp, axis=2, keepdims=True)
        probabilities = (weights_exp / mass).astype(jnp.bfloat16)
        context = jnp.einsum(
            "hqk,khe->qhe", probabilities, value_heads, preferred_element_type=jnp.float32
        )
        return (
            context.reshape(block_rows, head_count * head_width).astype(jnp.bfloat16),
            (row_max + jnp.log(mass))[:, :, 0],
        )

    contexts, log_mass = lax.map(
        one_block,
        (
            queries.reshape(block_count, block_rows, head_count * head_width),
            seg_ids.reshape(block_count, block_rows),
        ),
    )
    return (contexts.reshape(key_count, head_count * head_width), log_mass)


def attend_backward(
    queries, key_rows, value_rows, seg_ids, log_mass, grad_context, head_count, head_width
):
    key_count = key_rows.shape[0]
    block_rows = min(512, key_count)
    block_count = key_count // block_rows
    key_heads = key_rows.reshape(key_count, head_count, head_width)
    value_heads = value_rows.reshape(key_count, head_count, head_width)
    score_scale = 1.0 / math.sqrt(head_width)

    def one_block(carry, block_item):
        grad_keys, grad_values = carry
        query_block, block_ids, block_mass, grad_block = block_item
        query_heads = query_block.reshape(block_rows, head_count, head_width)
        grad_heads = grad_block.reshape(block_rows, head_count, head_width)
        scores = (
            jnp.einsum("qhe,khe->hqk", query_heads, key_heads, preferred_element_type=jnp.float32)
            * score_scale
        )
        allowed = (block_ids[:, None] == seg_ids[None, :])[None]
        probabilities = jnp.where(allowed, jnp.exp(scores - block_mass[:, :, None]), 0.0)
        rounded = probabilities.astype(jnp.bfloat16)
        grad_values = grad_values + jnp.einsum(
            "hqk,qhe->khe", rounded, grad_heads, preferred_element_type=jnp.float32
        )
        grad_probs = jnp.einsum(
            "qhe,khe->hqk", grad_heads, value_heads, preferred_element_type=jnp.float32
        )
        grad_scores = probabilities * (
            grad_probs - jnp.sum(probabilities * grad_probs, axis=2, keepdims=True)
        )
        grad_scores = grad_scores.astype(jnp.bfloat16)
        grad_query = (
            jnp.einsum("hqk,khe->qhe", grad_scores, key_heads, preferred_element_type=jnp.float32)
            * score_scale
        )
        grad_keys = (
            grad_keys
            + jnp.einsum(
                "hqk,qhe->khe", grad_scores, query_heads, preferred_element_type=jnp.float32
            )
            * score_scale
        )
        return ((grad_keys, grad_values), grad_query.reshape(block_rows, head_count * head_width))

    empty = jnp.zeros((key_count, head_count, head_width), jnp.float32)
    (grad_keys, grad_values), grad_queries = lax.scan(
        one_block,
        (empty, empty),
        (
            queries.reshape(block_count, block_rows, head_count * head_width),
            seg_ids.reshape(block_count, block_rows),
            log_mass,
            grad_context.reshape(block_count, block_rows, head_count * head_width),
        ),
    )
    width = head_count * head_width
    return (
        grad_queries.reshape(key_count, width).astype(jnp.bfloat16),
        grad_keys.reshape(key_count, width).astype(jnp.bfloat16),
        grad_values.reshape(key_count, width).astype(jnp.bfloat16),
    )


def local(
    tokens,
    seg_ids,
    query_weight,
    key_weight,
    value_weight,
    query_bias,
    value_bias,
    out_weight,
    out_bias,
    attention_norm_gain,
    attention_norm_shift,
    up_weight,
    up_bias,
    down_weight,
    down_bias,
    feedforward_norm_gain,
    feedforward_norm_shift,
    cotangent,
):
    head_width = HEAD_DIM
    head_count = query_weight.shape[1] // head_width
    valid_token_mask = (seg_ids >= 0)[:, None]
    queries = (
        jnp.dot(tokens, query_weight, preferred_element_type=jnp.float32) + query_bias
    ).astype(jnp.bfloat16)
    key_rows = jnp.dot(tokens, key_weight, preferred_element_type=jnp.float32).astype(jnp.bfloat16)
    value_rows = (
        jnp.dot(tokens, value_weight, preferred_element_type=jnp.float32) + value_bias
    ).astype(jnp.bfloat16)
    context, log_mass = attend_forward(
        queries, key_rows, value_rows, seg_ids, head_count, head_width
    )
    attn_sum = tensor_sum(dot_rows(context, out_weight))
    attention_residual = tokens.astype(jnp.float32) + attn_sum + out_bias
    centered_rows_first, inverse_deviation_first = apply_layer_norm(attention_residual)
    hidden_state = centered_rows_first * attention_norm_gain + attention_norm_shift
    hidden_low = hidden_state.astype(jnp.bfloat16)
    up_rows = jnp.dot(hidden_low, up_weight, preferred_element_type=jnp.float32) + up_bias
    act_low = jax.nn.gelu(up_rows, approximate=False).astype(jnp.bfloat16)
    down_sum = tensor_sum(dot_rows(act_low, down_weight))
    feedforward_residual = hidden_state + down_sum + down_bias
    centered_rows_second, inverse_deviation_second = apply_layer_norm(feedforward_residual)
    mixed = jnp.where(
        valid_token_mask, centered_rows_second * feedforward_norm_gain + feedforward_norm_shift, 0.0
    ).astype(jnp.bfloat16)
    incoming_gradient = jnp.where(valid_token_mask, cotangent.astype(jnp.float32), 0.0)
    grad_res_two, grad_gain_second, grad_shift_second = norm_backward_pass(
        incoming_gradient, centered_rows_second, inverse_deviation_second, feedforward_norm_gain
    )
    grad_down_low = grad_res_two.astype(jnp.bfloat16)
    grad_down_bias = jnp.sum(grad_down_low, axis=0, dtype=jnp.float32)
    down_share = dp_share_halves(grad_down_low, act_low)
    grad_act = jnp.dot(grad_down_low, down_weight, preferred_element_type=jnp.float32)
    normal_cdf = 0.5 * (1.0 + lax.erf(up_rows * (1.0 / math.sqrt(2.0))))
    normal_density = jnp.exp(-0.5 * up_rows * up_rows) * (1.0 / math.sqrt(2.0 * math.pi))
    grad_up_low = (grad_act * (normal_cdf + up_rows * normal_density)).astype(jnp.bfloat16)
    grad_up_bias = jnp.sum(grad_up_low, axis=0, dtype=jnp.float32)
    up_share = dp_share_halves(hidden_low, grad_up_low)
    back_sum = tensor_sum(dot_rows(grad_up_low, up_weight))
    hidden_gradient = grad_res_two + back_sum
    grad_res_one, grad_gain_first, grad_shift_first = norm_backward_pass(
        hidden_gradient, centered_rows_first, inverse_deviation_first, attention_norm_gain
    )
    grad_attn_low = grad_res_one.astype(jnp.bfloat16)
    grad_out_bias = jnp.sum(grad_attn_low, axis=0, dtype=jnp.float32)
    out_share = dp_share(grad_attn_low, context, upward)
    grad_context = jnp.dot(grad_attn_low, out_weight, preferred_element_type=jnp.float32).astype(
        jnp.bfloat16
    )
    grad_queries, grad_keys, grad_values = attend_backward(
        queries, key_rows, value_rows, seg_ids, log_mass, grad_context, head_count, head_width
    )
    grad_query_bias = jnp.sum(grad_queries, axis=0, dtype=jnp.float32)
    grad_value_bias = jnp.sum(grad_values, axis=0, dtype=jnp.float32)
    query_share = dp_share(tokens, grad_queries, upward)
    key_share = dp_share(tokens, grad_keys, rotated)
    value_share = dp_share(tokens, grad_values, rotated)
    input_part = (
        dot_rows(grad_queries, query_weight)
        + dot_rows(grad_keys, key_weight)
        + dot_rows(grad_values, value_weight)
    )
    grad_tokens = grad_res_one + tensor_sum(input_part)
    rows = [
        grad_query_bias,
        grad_value_bias,
        grad_up_bias,
        grad_out_bias,
        grad_gain_first,
        grad_shift_first,
        grad_down_bias,
        grad_gain_second,
        grad_shift_second,
    ]
    width = max(row.shape[0] for row in rows)
    line = lax.broadcasted_iota(jnp.int32, (len(rows), width), 0)
    stacked = jnp.zeros((len(rows), width), jnp.float32)
    for index, row in enumerate(rows):
        padded = jnp.pad(row, (0, width - row.shape[0]))
        stacked = jnp.where(line == index, padded[None, :], stacked)
    total = dp_sum(stacked)
    sums = [total[index, : row.shape[0]] for index, row in enumerate(rows)]
    (
        query_bias_sum,
        value_bias_sum,
        up_bias_sum,
        out_bias_sum,
        gain_first_sum,
        shift_first_sum,
        down_bias_sum,
        gain_second_sum,
        shift_second_sum,
    ) = sums
    return (
        mixed,
        grad_tokens,
        query_share,
        key_share,
        value_share,
        query_bias_sum,
        value_bias_sum,
        out_share,
        out_bias_sum,
        gain_first_sum,
        shift_first_sum,
        up_share,
        up_bias_sum,
        down_share,
        down_bias_sum,
        gain_second_sum,
        shift_second_sum,
    )


def solution(mesh):
    return jax.shard_map(
        local,
        mesh=mesh,
        in_specs=(
            P("dp", None),
            P("dp"),
            P(None, "tensor"),
            P(None, "tensor"),
            P(None, "tensor"),
            P("tensor"),
            P("tensor"),
            P(None, "tensor"),
            P(),
            P(),
            P(),
            P(None, "tensor"),
            P("tensor"),
            P(None, "tensor"),
            P(),
            P(),
            P(),
            P("dp", None),
        ),
        out_specs=(
            P("dp", None),
            P("dp", None),
            P("dp", "tensor"),
            P("dp", "tensor"),
            P("dp", "tensor"),
            P("tensor"),
            P("tensor"),
            P("dp", "tensor"),
            P(),
            P(),
            P(),
            P("dp", "tensor"),
            P("tensor"),
            P("dp", "tensor"),
            P(),
            P(),
            P(),
        ),
        check_vma=False,
    )
```

```python
import math

import jax
import jax.numpy as jnp
from jax import lax
from jax.sharding import PartitionSpec as P

HEAD_DIM = 64


epsilon = 1e-12
masked_value = -1e30


def dot_rows(left, right):
    return lax.dot_general(
        left, right, (((1,), (1,)), ((), ())), preferred_element_type=jnp.float32
    )


def dot_cols(left, right):
    return lax.dot_general(
        left, right, (((0,), (0,)), ((), ())), preferred_element_type=jnp.float32
    )


def tensor_sum(part):
    size = lax.axis_size("tensor")
    if size != 2:
        return lax.psum(part, "tensor")
    return part + lax.ppermute(part, "tensor", [(0, 1), (1, 0)])


def dp_sum(part):
    size = lax.axis_size("dp")
    if size & (size - 1):
        return lax.psum(part, "dp")
    step = 1
    while step < size:
        part = part + lax.ppermute(part, "dp", [(i, i ^ step) for i in range(size)])
        step *= 2
    return part


def dp_share_open(left, right, rotate):
    size = lax.axis_size("dp")
    count = size.bit_length() - 1
    if size != 1 << count:
        share = lax.psum_scatter(dot_cols(left, right), "dp", scatter_dimension=0, tiled=True)
        return (share, [], [])
    tokens, width = right.shape
    rows = left.shape[1] // size
    axes = list(range(count - 1, -1, -1))
    order = list(range(count))
    if rotate:
        order = order[:1] + order[2:] + order[1:2]
    blocks = left.T.reshape((2,) * count + (rows, tokens))
    halves = [
        jnp.dot(half.reshape(-1, tokens), right, preferred_element_type=jnp.float32).reshape(
            (2,) * (count - 1) + (rows, width)
        )
        for half in split_halves(blocks, axes, order[0])
    ]
    return exchange(halves, axes, order)


def split_halves(part, axes, bit):
    mine = (lax.axis_index("dp") >> bit) & 1
    axis = axes.index(bit)
    return (
        lax.dynamic_index_in_dim(part, 1 - mine, axis, keepdims=False),
        lax.dynamic_index_in_dim(part, mine, axis, keepdims=False),
    )


def exchange(halves, axes, order):
    send, keep = halves
    bit = order[0]
    pairs = [(i, i ^ (1 << bit)) for i in range(lax.axis_size("dp"))]
    part = keep + lax.ppermute(send, "dp", pairs)
    return (part, [axis for axis in axes if axis != bit], order[1:])


def dp_share_step(state):
    part, axes, order = state
    if not order:
        return state
    return exchange(split_halves(part, axes, order[0]), axes, order)


def dp_share_close(state):
    while state[2]:
        state = dp_share_step(state)
    return state[0]


def after(values, states):
    values, parts = lax.optimization_barrier((values, [state[0] for state in states]))
    return (values, [(part, *state[1:]) for part, state in zip(parts, states)])


def open_halves(left, right):
    middle = right.shape[1] // 2
    return [
        dp_share_open(left, right[:, :middle], False),
        dp_share_open(left, right[:, middle:], True),
    ]


def apply_layer_norm(rows):
    row_mean = jnp.mean(rows, axis=1, keepdims=True)
    centred = rows - row_mean
    inverse_deviation = lax.rsqrt(jnp.mean(centred * centred, axis=1, keepdims=True) + epsilon)
    return (centred * inverse_deviation, inverse_deviation)


def norm_backward_pass(incoming_gradient, centered_rows, inverse_deviation, norm_gain):
    scaled_rows = incoming_gradient * norm_gain
    row_gradient = inverse_deviation * (
        scaled_rows
        - jnp.mean(scaled_rows, axis=1, keepdims=True)
        - centered_rows * jnp.mean(scaled_rows * centered_rows, axis=1, keepdims=True)
    )
    return (
        row_gradient,
        jnp.sum(incoming_gradient * centered_rows, axis=0),
        jnp.sum(incoming_gradient, axis=0),
    )


def attend_forward(queries, key_rows, value_rows, seg_ids, head_count, head_width):
    key_count = key_rows.shape[0]
    block_rows = min(512, key_count)
    block_count = key_count // block_rows
    key_heads = key_rows.reshape(key_count, head_count, head_width)
    value_heads = value_rows.reshape(key_count, head_count, head_width)
    score_scale = 1.0 / math.sqrt(head_width)

    def one_block(block_item):
        query_block, block_ids = block_item
        query_heads = query_block.reshape(block_rows, head_count, head_width)
        scores = (
            jnp.einsum("qhe,khe->hqk", query_heads, key_heads, preferred_element_type=jnp.float32)
            * score_scale
        )
        allowed = (block_ids[:, None] == seg_ids[None, :])[None]
        scores = jnp.where(allowed, scores, masked_value)
        row_max = jnp.max(scores, axis=2, keepdims=True)
        weights_exp = jnp.exp(scores - row_max)
        mass = jnp.sum(weights_exp, axis=2, keepdims=True)
        probabilities = (weights_exp / mass).astype(jnp.bfloat16)
        context = jnp.einsum(
            "hqk,khe->qhe", probabilities, value_heads, preferred_element_type=jnp.float32
        )
        return (
            context.reshape(block_rows, head_count * head_width).astype(jnp.bfloat16),
            (row_max + jnp.log(mass))[:, :, 0],
        )

    contexts, log_mass = lax.map(
        one_block,
        (
            queries.reshape(block_count, block_rows, head_count * head_width),
            seg_ids.reshape(block_count, block_rows),
        ),
    )
    return (contexts.reshape(key_count, head_count * head_width), log_mass)


def attend_backward(
    queries, key_rows, value_rows, seg_ids, log_mass, grad_context, head_count, head_width
):
    key_count = key_rows.shape[0]
    block_rows = min(512, key_count)
    block_count = key_count // block_rows
    key_heads = key_rows.reshape(key_count, head_count, head_width)
    value_heads = value_rows.reshape(key_count, head_count, head_width)
    score_scale = 1.0 / math.sqrt(head_width)

    def one_block(carry, block_item):
        grad_keys, grad_values = carry
        query_block, block_ids, block_mass, grad_block = block_item
        query_heads = query_block.reshape(block_rows, head_count, head_width)
        grad_heads = grad_block.reshape(block_rows, head_count, head_width)
        scores = (
            jnp.einsum("qhe,khe->hqk", query_heads, key_heads, preferred_element_type=jnp.float32)
            * score_scale
        )
        allowed = (block_ids[:, None] == seg_ids[None, :])[None]
        probabilities = jnp.where(allowed, jnp.exp(scores - block_mass[:, :, None]), 0.0)
        rounded = probabilities.astype(jnp.bfloat16)
        grad_values = grad_values + jnp.einsum(
            "hqk,qhe->khe", rounded, grad_heads, preferred_element_type=jnp.float32
        )
        grad_probs = jnp.einsum(
            "qhe,khe->hqk", grad_heads, value_heads, preferred_element_type=jnp.float32
        )
        grad_scores = probabilities * (
            grad_probs - jnp.sum(probabilities * grad_probs, axis=2, keepdims=True)
        )
        grad_scores = grad_scores.astype(jnp.bfloat16)
        grad_query = (
            jnp.einsum("hqk,khe->qhe", grad_scores, key_heads, preferred_element_type=jnp.float32)
            * score_scale
        )
        grad_keys = (
            grad_keys
            + jnp.einsum(
                "hqk,qhe->khe", grad_scores, query_heads, preferred_element_type=jnp.float32
            )
            * score_scale
        )
        return ((grad_keys, grad_values), grad_query.reshape(block_rows, head_count * head_width))

    empty = jnp.zeros((key_count, head_count, head_width), jnp.float32)
    (grad_keys, grad_values), grad_queries = lax.scan(
        one_block,
        (empty, empty),
        (
            queries.reshape(block_count, block_rows, head_count * head_width),
            seg_ids.reshape(block_count, block_rows),
            log_mass,
            grad_context.reshape(block_count, block_rows, head_count * head_width),
        ),
    )
    width = head_count * head_width
    return (
        grad_queries.reshape(key_count, width).astype(jnp.bfloat16),
        grad_keys.reshape(key_count, width).astype(jnp.bfloat16),
        grad_values.reshape(key_count, width).astype(jnp.bfloat16),
    )


def local(
    tokens,
    seg_ids,
    query_weight,
    key_weight,
    value_weight,
    query_bias,
    value_bias,
    out_weight,
    out_bias,
    attention_norm_gain,
    attention_norm_shift,
    up_weight,
    up_bias,
    down_weight,
    down_bias,
    feedforward_norm_gain,
    feedforward_norm_shift,
    cotangent,
):
    head_width = HEAD_DIM
    head_count = query_weight.shape[1] // head_width
    valid_token_mask = (seg_ids >= 0)[:, None]
    queries = (
        jnp.dot(tokens, query_weight, preferred_element_type=jnp.float32) + query_bias
    ).astype(jnp.bfloat16)
    key_rows = jnp.dot(tokens, key_weight, preferred_element_type=jnp.float32).astype(jnp.bfloat16)
    value_rows = (
        jnp.dot(tokens, value_weight, preferred_element_type=jnp.float32) + value_bias
    ).astype(jnp.bfloat16)
    context, log_mass = attend_forward(
        queries, key_rows, value_rows, seg_ids, head_count, head_width
    )
    attn_sum = tensor_sum(dot_rows(context, out_weight))
    attention_residual = tokens.astype(jnp.float32) + attn_sum + out_bias
    centered_rows_first, inverse_deviation_first = apply_layer_norm(attention_residual)
    hidden_state = centered_rows_first * attention_norm_gain + attention_norm_shift
    hidden_low = hidden_state.astype(jnp.bfloat16)
    up_rows = jnp.dot(hidden_low, up_weight, preferred_element_type=jnp.float32) + up_bias
    act_low = jax.nn.gelu(up_rows, approximate=False).astype(jnp.bfloat16)
    down_sum = tensor_sum(dot_rows(act_low, down_weight))
    feedforward_residual = hidden_state + down_sum + down_bias
    centered_rows_second, inverse_deviation_second = apply_layer_norm(feedforward_residual)
    mixed = jnp.where(
        valid_token_mask, centered_rows_second * feedforward_norm_gain + feedforward_norm_shift, 0.0
    ).astype(jnp.bfloat16)
    incoming_gradient = jnp.where(valid_token_mask, cotangent.astype(jnp.float32), 0.0)
    grad_res_two, grad_gain_second, grad_shift_second = norm_backward_pass(
        incoming_gradient, centered_rows_second, inverse_deviation_second, feedforward_norm_gain
    )
    grad_down_low = grad_res_two.astype(jnp.bfloat16)
    grad_down_bias = jnp.sum(grad_down_low, axis=0, dtype=jnp.float32)
    down_states = open_halves(grad_down_low, act_low)
    grad_act = jnp.dot(grad_down_low, down_weight, preferred_element_type=jnp.float32)
    normal_cdf = 0.5 * (1.0 + lax.erf(up_rows * (1.0 / math.sqrt(2.0))))
    normal_density = jnp.exp(-0.5 * up_rows * up_rows) * (1.0 / math.sqrt(2.0 * math.pi))
    grad_up_low = (grad_act * (normal_cdf + up_rows * normal_density)).astype(jnp.bfloat16)
    grad_up_bias = jnp.sum(grad_up_low, axis=0, dtype=jnp.float32)
    up_states = open_halves(hidden_low, grad_up_low)
    back_sum = tensor_sum(dot_rows(grad_up_low, up_weight))
    hidden_gradient = grad_res_two + back_sum
    grad_res_one, grad_gain_first, grad_shift_first = norm_backward_pass(
        hidden_gradient, centered_rows_first, inverse_deviation_first, attention_norm_gain
    )
    grad_attn_low, down_states = after(grad_res_one.astype(jnp.bfloat16), down_states)
    down_states = [dp_share_step(state) for state in down_states]
    grad_out_bias = jnp.sum(grad_attn_low, axis=0, dtype=jnp.float32)
    out_state = dp_share_open(grad_attn_low, context, False)
    grad_context = jnp.dot(grad_attn_low, out_weight, preferred_element_type=jnp.float32).astype(
        jnp.bfloat16
    )
    grad_context, up_states = after(grad_context, up_states)
    up_states = [dp_share_step(state) for state in up_states]
    attention_gradients = attend_backward(
        queries, key_rows, value_rows, seg_ids, log_mass, grad_context, head_count, head_width
    )
    (grad_queries, grad_keys, grad_values), (out_state, *down_states) = after(
        attention_gradients, [out_state, *down_states]
    )
    grad_query_bias = jnp.sum(grad_queries, axis=0, dtype=jnp.float32)
    grad_value_bias = jnp.sum(grad_values, axis=0, dtype=jnp.float32)
    query_share = dp_share_close(dp_share_open(tokens, grad_queries, False))
    key_share = dp_share_close(dp_share_open(tokens, grad_keys, True))
    late_values, up_states = after(grad_values, up_states)
    value_share = dp_share_close(dp_share_open(tokens, late_values, True))
    out_share = dp_share_close(out_state)
    down_share = jnp.concatenate([dp_share_close(state) for state in down_states], axis=1)
    up_share = jnp.concatenate([dp_share_close(state) for state in up_states], axis=1)
    input_part = (
        dot_rows(grad_queries, query_weight)
        + dot_rows(grad_keys, key_weight)
        + dot_rows(grad_values, value_weight)
    )
    grad_tokens = grad_res_one + tensor_sum(input_part)
    rows = [
        grad_query_bias,
        grad_value_bias,
        grad_up_bias,
        grad_out_bias,
        grad_gain_first,
        grad_shift_first,
        grad_down_bias,
        grad_gain_second,
        grad_shift_second,
    ]
    width = max(row.shape[0] for row in rows)
    line = lax.broadcasted_iota(jnp.int32, (len(rows), width), 0)
    stacked = jnp.zeros((len(rows), width), jnp.float32)
    for index, row in enumerate(rows):
        padded = jnp.pad(row, (0, width - row.shape[0]))
        stacked = jnp.where(line == index, padded[None, :], stacked)
    total = dp_sum(stacked)
    sums = [total[index, : row.shape[0]] for index, row in enumerate(rows)]
    (
        query_bias_sum,
        value_bias_sum,
        up_bias_sum,
        out_bias_sum,
        gain_first_sum,
        shift_first_sum,
        down_bias_sum,
        gain_second_sum,
        shift_second_sum,
    ) = sums
    return (
        mixed,
        grad_tokens,
        query_share,
        key_share,
        value_share,
        query_bias_sum,
        value_bias_sum,
        out_share,
        out_bias_sum,
        gain_first_sum,
        shift_first_sum,
        up_share,
        up_bias_sum,
        down_share,
        down_bias_sum,
        gain_second_sum,
        shift_second_sum,
    )


def solution(mesh):
    return jax.shard_map(
        local,
        mesh=mesh,
        in_specs=(
            P("dp", None),
            P("dp"),
            P(None, "tensor"),
            P(None, "tensor"),
            P(None, "tensor"),
            P("tensor"),
            P("tensor"),
            P(None, "tensor"),
            P(),
            P(),
            P(),
            P(None, "tensor"),
            P("tensor"),
            P(None, "tensor"),
            P(),
            P(),
            P(),
            P("dp", None),
        ),
        out_specs=(
            P("dp", None),
            P("dp", None),
            P("dp", "tensor"),
            P("dp", "tensor"),
            P("dp", "tensor"),
            P("tensor"),
            P("tensor"),
            P("dp", "tensor"),
            P(),
            P(),
            P(),
            P("dp", "tensor"),
            P("tensor"),
            P("dp", "tensor"),
            P(),
            P(),
            P(),
        ),
        check_vma=False,
    )
```

```python
import math

import jax
import jax.numpy as jnp
from jax import lax
from jax.sharding import PartitionSpec as P

HEAD_DIM = 64


epsilon = 1e-12
masked_value = -1e30


def dot_rows(left, right):
    return lax.dot_general(
        left, right, (((1,), (1,)), ((), ())), preferred_element_type=jnp.float32
    )


def dot_cols(left, right):
    return lax.dot_general(
        left, right, (((0,), (0,)), ((), ())), preferred_element_type=jnp.float32
    )


def tensor_sum(part):
    size = lax.axis_size("tensor")
    if size != 2:
        return lax.psum(part, "tensor")
    return part + lax.ppermute(part, "tensor", [(0, 1), (1, 0)])


def dp_sum(part):
    size = lax.axis_size("dp")
    if size & (size - 1):
        return lax.psum(part, "dp")
    step = 1
    while step < size:
        part = part + lax.ppermute(part, "dp", [(i, i ^ step) for i in range(size)])
        step *= 2
    return part


def dp_share_open(left, right, rotate):
    size = lax.axis_size("dp")
    count = size.bit_length() - 1
    if size != 1 << count:
        share = lax.psum_scatter(dot_cols(left, right), "dp", scatter_dimension=0, tiled=True)
        return (share, [], [])
    tokens, width = right.shape
    rows = left.shape[1] // size
    axes = list(range(count - 1, -1, -1))
    order = list(range(count))
    if rotate:
        order = order[:1] + order[2:] + order[1:2]
    blocks = left.T.reshape((2,) * count + (rows, tokens))
    halves = [
        jnp.dot(half.reshape(-1, tokens), right, preferred_element_type=jnp.float32).reshape(
            (2,) * (count - 1) + (rows, width)
        )
        for half in split_halves(blocks, axes, order[0])
    ]
    return exchange(halves, axes, order)


def split_halves(part, axes, bit):
    mine = (lax.axis_index("dp") >> bit) & 1
    axis = axes.index(bit)
    return (
        lax.dynamic_index_in_dim(part, 1 - mine, axis, keepdims=False),
        lax.dynamic_index_in_dim(part, mine, axis, keepdims=False),
    )


def exchange(halves, axes, order):
    send, keep = halves
    bit = order[0]
    pairs = [(i, i ^ (1 << bit)) for i in range(lax.axis_size("dp"))]
    part = keep + lax.ppermute(send, "dp", pairs)
    return (part, [axis for axis in axes if axis != bit], order[1:])


def dp_share_step(state):
    part, axes, order = state
    if not order:
        return state
    return exchange(split_halves(part, axes, order[0]), axes, order)


def dp_share_close(state):
    while state[2]:
        state = dp_share_step(state)
    return state[0]


def after(values, states):
    values, parts = lax.optimization_barrier((values, [state[0] for state in states]))
    return (values, [(part, *state[1:]) for part, state in zip(parts, states)])


def open_halves(left, right):
    middle = right.shape[1] // 2
    return [
        dp_share_open(left, right[:, :middle], False),
        dp_share_open(left, right[:, middle:], True),
    ]


def apply_layer_norm(rows):
    row_mean = jnp.mean(rows, axis=1, keepdims=True)
    centred = rows - row_mean
    inverse_deviation = lax.rsqrt(jnp.mean(centred * centred, axis=1, keepdims=True) + epsilon)
    return (centred * inverse_deviation, inverse_deviation)


def norm_backward_pass(incoming_gradient, centered_rows, inverse_deviation, norm_gain):
    scaled_rows = incoming_gradient * norm_gain
    row_gradient = inverse_deviation * (
        scaled_rows
        - jnp.mean(scaled_rows, axis=1, keepdims=True)
        - centered_rows * jnp.mean(scaled_rows * centered_rows, axis=1, keepdims=True)
    )
    return (
        row_gradient,
        jnp.sum(incoming_gradient * centered_rows, axis=0),
        jnp.sum(incoming_gradient, axis=0),
    )


def attend_forward(queries, key_rows, value_rows, seg_ids, head_count, head_width):
    key_count = key_rows.shape[0]
    block_rows = min(512, key_count)
    block_count = key_count // block_rows
    key_heads = key_rows.reshape(key_count, head_count, head_width)
    value_heads = value_rows.reshape(key_count, head_count, head_width)
    score_scale = 1.0 / math.sqrt(head_width)

    def one_block(block_item):
        query_block, block_ids = block_item
        query_heads = query_block.reshape(block_rows, head_count, head_width)
        scores = (
            jnp.einsum("qhe,khe->hqk", query_heads, key_heads, preferred_element_type=jnp.float32)
            * score_scale
        )
        allowed = (block_ids[:, None] == seg_ids[None, :])[None]
        scores = jnp.where(allowed, scores, masked_value)
        row_max = jnp.max(scores, axis=2, keepdims=True)
        weights_exp = jnp.exp(scores - row_max)
        mass = jnp.sum(weights_exp, axis=2, keepdims=True)
        probabilities = (weights_exp / mass).astype(jnp.bfloat16)
        context = jnp.einsum(
            "hqk,khe->qhe", probabilities, value_heads, preferred_element_type=jnp.float32
        )
        return (
            context.reshape(block_rows, head_count * head_width).astype(jnp.bfloat16),
            (row_max + jnp.log(mass))[:, :, 0],
        )

    contexts, log_mass = lax.map(
        one_block,
        (
            queries.reshape(block_count, block_rows, head_count * head_width),
            seg_ids.reshape(block_count, block_rows),
        ),
    )
    return (contexts.reshape(key_count, head_count * head_width), log_mass)


def attend_backward(
    queries, key_rows, value_rows, seg_ids, log_mass, grad_context, head_count, head_width
):
    key_count = key_rows.shape[0]
    block_rows = min(512, key_count)
    block_count = key_count // block_rows
    key_heads = key_rows.reshape(key_count, head_count, head_width)
    value_heads = value_rows.reshape(key_count, head_count, head_width)
    score_scale = 1.0 / math.sqrt(head_width)

    def one_block(carry, block_item):
        grad_keys, grad_values = carry
        query_block, block_ids, block_mass, grad_block = block_item
        query_heads = query_block.reshape(block_rows, head_count, head_width)
        grad_heads = grad_block.reshape(block_rows, head_count, head_width)
        scores = (
            jnp.einsum("qhe,khe->hqk", query_heads, key_heads, preferred_element_type=jnp.float32)
            * score_scale
        )
        allowed = (block_ids[:, None] == seg_ids[None, :])[None]
        probabilities = jnp.where(allowed, jnp.exp(scores - block_mass[:, :, None]), 0.0)
        rounded = probabilities.astype(jnp.bfloat16)
        grad_values = grad_values + jnp.einsum(
            "hqk,qhe->khe", rounded, grad_heads, preferred_element_type=jnp.float32
        )
        grad_probs = jnp.einsum(
            "qhe,khe->hqk", grad_heads, value_heads, preferred_element_type=jnp.float32
        )
        grad_scores = probabilities * (
            grad_probs - jnp.sum(probabilities * grad_probs, axis=2, keepdims=True)
        )
        grad_scores = grad_scores.astype(jnp.bfloat16)
        grad_query = (
            jnp.einsum("hqk,khe->qhe", grad_scores, key_heads, preferred_element_type=jnp.float32)
            * score_scale
        )
        grad_keys = (
            grad_keys
            + jnp.einsum(
                "hqk,qhe->khe", grad_scores, query_heads, preferred_element_type=jnp.float32
            )
            * score_scale
        )
        return ((grad_keys, grad_values), grad_query.reshape(block_rows, head_count * head_width))

    empty = jnp.zeros((key_count, head_count, head_width), jnp.float32)
    (grad_keys, grad_values), grad_queries = lax.scan(
        one_block,
        (empty, empty),
        (
            queries.reshape(block_count, block_rows, head_count * head_width),
            seg_ids.reshape(block_count, block_rows),
            log_mass,
            grad_context.reshape(block_count, block_rows, head_count * head_width),
        ),
    )
    width = head_count * head_width
    return (
        grad_queries.reshape(key_count, width).astype(jnp.bfloat16),
        grad_keys.reshape(key_count, width).astype(jnp.bfloat16),
        grad_values.reshape(key_count, width).astype(jnp.bfloat16),
    )


def local(
    tokens,
    seg_ids,
    query_weight,
    key_weight,
    value_weight,
    query_bias,
    value_bias,
    out_weight,
    out_bias,
    attention_norm_gain,
    attention_norm_shift,
    up_weight,
    up_bias,
    down_weight,
    down_bias,
    feedforward_norm_gain,
    feedforward_norm_shift,
    cotangent,
):
    head_width = HEAD_DIM
    head_count = query_weight.shape[1] // head_width
    valid_token_mask = (seg_ids >= 0)[:, None]
    queries = (
        jnp.dot(tokens, query_weight, preferred_element_type=jnp.float32) + query_bias
    ).astype(jnp.bfloat16)
    key_rows = jnp.dot(tokens, key_weight, preferred_element_type=jnp.float32).astype(jnp.bfloat16)
    value_rows = (
        jnp.dot(tokens, value_weight, preferred_element_type=jnp.float32) + value_bias
    ).astype(jnp.bfloat16)
    context, log_mass = attend_forward(
        queries, key_rows, value_rows, seg_ids, head_count, head_width
    )
    attn_sum = tensor_sum(dot_rows(context, out_weight))
    attention_residual = tokens.astype(jnp.float32) + attn_sum + out_bias
    centered_rows_first, inverse_deviation_first = apply_layer_norm(attention_residual)
    hidden_state = centered_rows_first * attention_norm_gain + attention_norm_shift
    hidden_low = hidden_state.astype(jnp.bfloat16)
    up_rows = jnp.dot(hidden_low, up_weight, preferred_element_type=jnp.float32) + up_bias
    act_low = jax.nn.gelu(up_rows, approximate=False).astype(jnp.bfloat16)
    down_sum = tensor_sum(dot_rows(act_low, down_weight))
    feedforward_residual = hidden_state + down_sum + down_bias
    centered_rows_second, inverse_deviation_second = apply_layer_norm(feedforward_residual)
    mixed = jnp.where(
        valid_token_mask, centered_rows_second * feedforward_norm_gain + feedforward_norm_shift, 0.0
    ).astype(jnp.bfloat16)
    incoming_gradient = jnp.where(valid_token_mask, cotangent.astype(jnp.float32), 0.0)
    grad_res_two, grad_gain_second, grad_shift_second = norm_backward_pass(
        incoming_gradient, centered_rows_second, inverse_deviation_second, feedforward_norm_gain
    )
    grad_down_low = grad_res_two.astype(jnp.bfloat16)
    grad_down_bias = jnp.sum(grad_down_low, axis=0, dtype=jnp.float32)
    down_states = open_halves(grad_down_low, act_low)
    grad_act = jnp.dot(grad_down_low, down_weight, preferred_element_type=jnp.float32)
    normal_cdf = 0.5 * (1.0 + lax.erf(up_rows * (1.0 / math.sqrt(2.0))))
    normal_density = jnp.exp(-0.5 * up_rows * up_rows) * (1.0 / math.sqrt(2.0 * math.pi))
    grad_up_low = (grad_act * (normal_cdf + up_rows * normal_density)).astype(jnp.bfloat16)
    grad_up_bias = jnp.sum(grad_up_low, axis=0, dtype=jnp.float32)
    up_states = open_halves(hidden_low, grad_up_low)
    back_sum = tensor_sum(dot_rows(grad_up_low, up_weight))
    hidden_gradient = grad_res_two + back_sum
    grad_res_one, grad_gain_first, grad_shift_first = norm_backward_pass(
        hidden_gradient, centered_rows_first, inverse_deviation_first, attention_norm_gain
    )
    grad_attn_low, down_states = after(grad_res_one.astype(jnp.bfloat16), down_states)
    down_states = [dp_share_step(state) for state in down_states]
    grad_out_bias = jnp.sum(grad_attn_low, axis=0, dtype=jnp.float32)
    out_state = dp_share_open(grad_attn_low, context, False)
    grad_context = jnp.dot(grad_attn_low, out_weight, preferred_element_type=jnp.float32).astype(
        jnp.bfloat16
    )
    grad_context, up_states = after(grad_context, up_states)
    up_states = [dp_share_step(state) for state in up_states]
    attention_gradients = attend_backward(
        queries, key_rows, value_rows, seg_ids, log_mass, grad_context, head_count, head_width
    )
    (grad_queries, grad_keys, grad_values), (out_state, *down_states) = after(
        attention_gradients, [out_state, *down_states]
    )
    grad_query_bias = jnp.sum(grad_queries, axis=0, dtype=jnp.float32)
    grad_value_bias = jnp.sum(grad_values, axis=0, dtype=jnp.float32)
    query_state = dp_share_open(tokens, grad_queries, False)
    key_state = dp_share_open(tokens, grad_keys, True)
    value_state = dp_share_open(tokens, grad_values, True)
    input_part = (
        dot_rows(grad_queries, query_weight)
        + dot_rows(grad_keys, key_weight)
        + dot_rows(grad_values, value_weight)
    )
    grad_tokens = grad_res_one + tensor_sum(input_part)
    rows = [
        grad_query_bias,
        grad_value_bias,
        grad_up_bias,
        grad_out_bias,
        grad_gain_first,
        grad_shift_first,
        grad_down_bias,
        grad_gain_second,
        grad_shift_second,
    ]
    width = max(row.shape[0] for row in rows)
    line = lax.broadcasted_iota(jnp.int32, (len(rows), width), 0)
    stacked = jnp.zeros((len(rows), width), jnp.float32)
    for index, row in enumerate(rows):
        padded = jnp.pad(row, (0, width - row.shape[0]))
        stacked = jnp.where(line == index, padded[None, :], stacked)
    stacked, (query_state, key_state, value_state, *up_states) = after(
        stacked, [query_state, key_state, value_state, *up_states]
    )
    query_share = dp_share_close(query_state)
    key_share = dp_share_close(key_state)
    value_share = dp_share_close(value_state)
    out_share = dp_share_close(out_state)
    down_share = jnp.concatenate([dp_share_close(state) for state in down_states], axis=1)
    up_share = jnp.concatenate([dp_share_close(state) for state in up_states], axis=1)
    total = dp_sum(stacked)
    sums = [total[index, : row.shape[0]] for index, row in enumerate(rows)]
    (
        query_bias_sum,
        value_bias_sum,
        up_bias_sum,
        out_bias_sum,
        gain_first_sum,
        shift_first_sum,
        down_bias_sum,
        gain_second_sum,
        shift_second_sum,
    ) = sums
    return (
        mixed,
        grad_tokens,
        query_share,
        key_share,
        value_share,
        query_bias_sum,
        value_bias_sum,
        out_share,
        out_bias_sum,
        gain_first_sum,
        shift_first_sum,
        up_share,
        up_bias_sum,
        down_share,
        down_bias_sum,
        gain_second_sum,
        shift_second_sum,
    )


def solution(mesh):
    return jax.shard_map(
        local,
        mesh=mesh,
        in_specs=(
            P("dp", None),
            P("dp"),
            P(None, "tensor"),
            P(None, "tensor"),
            P(None, "tensor"),
            P("tensor"),
            P("tensor"),
            P(None, "tensor"),
            P(),
            P(),
            P(),
            P(None, "tensor"),
            P("tensor"),
            P(None, "tensor"),
            P(),
            P(),
            P(),
            P("dp", None),
        ),
        out_specs=(
            P("dp", None),
            P("dp", None),
            P("dp", "tensor"),
            P("dp", "tensor"),
            P("dp", "tensor"),
            P("tensor"),
            P("tensor"),
            P("dp", "tensor"),
            P(),
            P(),
            P(),
            P("dp", "tensor"),
            P("tensor"),
            P("dp", "tensor"),
            P(),
            P(),
            P(),
        ),
        check_vma=False,
    )
```
